32 devices in a mesh: groups: 2 (over y), beam: 8 (over z, x), mp: 2 (over core).
Axes of the slice: x: 2, y: 2, z: 4, core: 2. Of those that a mesh axis runs over, the one named last changes fastest.
Arguments:
- states: float32 [64, 8, 128, 128], P(('groups', 'beam'), 'mp'), parts along dimension 0, may hold values from -4 to 4
- parent_beam: int32 [64], P(('groups', 'beam')), parts along dimension 0, may hold values from 0 to 7, as said below
- next_token: int32 [64], P(('groups', 'beam')), parts along dimension 0, may hold values from 0 to 1023
- proj_table: bfloat16 [1024, 8, 640], P('beam', 'mp'), may hold values from -6 to 6
- gate_table: bfloat16 [1024, 3, 8], P('beam', None, 'mp'), may hold values from -6 to 6
- gain: float32 [8, 128], P('mp'), may hold values from 0.1 to 1.9
Outputs:
- readout: bfloat16 [64, 8, 128], P(('groups', 'beam'), 'mp'), parts along dimension 0
- new_states: float32 [64, 8, 128, 128], P(('groups', 'beam'), 'mp'), parts along dimension 0
The draws below stay inside these ranges and needn't reach their ends.
There are 2 independent parts, one for each index of `groups`. The reference program is written for one: setup_inputs(seed, part) draws one part's arguments, and reference() takes and returns one part's arrays. A program takes and returns all parts, laid end to end along the dimension named above; an argument that names none is the same for every part. Nothing has to cross between parts.
Inputs may be any that keep to these rules, and one draw needn't show every extreme that they name: The parent of hypothesis h = b * 4 + u is parent_beam[h] * 4 + u. In each aligned block of 4 hypotheses at most 2 take their parent from any one beam other than their own beam, and every block has a beam that supplies exactly 2.
All inputs are finite; a program needn't handle non-finite values.
Results may differ from the reference program's by a relative error of at most 0.001.
Values may be sent and summed in bfloat16 or wider, within the bound.
No kernel may reach another device: no remote copies, remote signals or barrier semaphores. Data moves between devices by JAX's collectives and lax.ppermute only.
A program may use at most 64 MiB of HBM per device.

```python
import math
import jax
import jax.numpy as jnp
import numpy as np
from jax import lax

HEADS = 8
HEAD_DIM = 128
BEAMS = 8
CAP = 2
HYP_DEV = 4
HYPS = 32
UTTS = 4
VOCAB = 1024


def draw_parent_beam(key, part):
    block_count = HYPS // HYP_DEV

    def draw_block(block_key, block_index):
        key_forced, key_pool, key_place = jax.random.split(block_key, 3)
        forced = jax.random.randint(key_forced, (), 1, BEAMS)
        offset_pool = jnp.concatenate([jnp.zeros((HYP_DEV,), jnp.int32), jnp.repeat(jnp.arange(1, BEAMS, dtype=jnp.int32), CAP)])
        shuffled = offset_pool[jax.random.permutation(key_pool, offset_pool.shape[0])]
        ordering = jnp.argsort((shuffled == forced).astype(jnp.int32), stable=True)
        remaining = shuffled[ordering][:HYP_DEV - CAP]
        offsets = jnp.concatenate([jnp.full((CAP,), forced, jnp.int32), remaining])
        offsets = offsets[jax.random.permutation(key_place, HYP_DEV)]
        own_beam = block_index * HYP_DEV // UTTS
        return ((own_beam - offsets) % BEAMS).astype(jnp.int32)
    block_keys = jax.random.split(jax.random.fold_in(key, 11), block_count)
    drawn = jax.vmap(draw_block)(block_keys, jnp.arange(block_count, dtype=jnp.int32))
    return drawn.reshape(HYPS).astype(jnp.int32)


def plant(values, rng, low, high):
    extent = values.shape
    place = [jax.random.randint(jax.random.fold_in(rng, axis), (), 0, extent[axis]) for axis in range(len(extent))]
    values = values.at[tuple(place)].set(low)
    longest = extent.index(max(extent))
    place[longest] = (place[longest] + 1) % extent[longest]
    return values.at[tuple(place)].set(high)


def block_levels(key, extent, shards, smallest, largest):
    level = 1.0
    for axis_at, blocks in shards:
        draws = jax.random.uniform(jax.random.fold_in(jax.random.fold_in(key, 6), axis_at), (blocks,), jnp.float32, smallest / len(shards), largest / len(shards))
        level = level * jnp.repeat(jnp.exp(draws), extent[axis_at] // blocks).reshape((-1,) + (1,) * (len(extent) - 1 - axis_at))
    return level


def rank_table(amount, lean):
    loads = [(1 << 20) // math.isqrt(grade ** lean) + 1 for grade in range(1, amount + 1)]
    deviation = 1 + sum(loads) // (1 << 30)
    return np.cumsum(np.array([max(1, weight // deviation) for weight in loads]))


def ranked_ids(key, dims, amount, slope):
    table = rank_table(amount, slope)
    ticket = jax.random.randint(jax.random.fold_in(key, 1), dims, 0, int(table[amount - 1]))
    grade = jnp.searchsorted(jnp.asarray(table, jnp.int32), ticket, side="right")
    return jax.random.permutation(jax.random.fold_in(key, 2), amount)[grade].astype(jnp.int32)


def gaussian(rng, extent, spread, limit, cuts=(), kind=jnp.bfloat16):
    level = block_levels(rng, extent, cuts, -0.22, 0.18) if cuts else 1.0
    values = jax.random.normal(rng, extent, jnp.float32) * spread * level
    return jnp.minimum(jnp.maximum(values, -limit), limit).astype(kind)


def setup_inputs(seed: int = 0, part: int = 0) -> dict:
    key_of = jax.random.split(jax.random.key(seed), 7)
    part_keys = jax.random.split(jax.random.fold_in(key_of[6], part), 7)
    states = gaussian(part_keys[0], (HYPS, HEADS, HEAD_DIM, HEAD_DIM), 0.5, 4.0, ((0, 8), (1, 2)), jnp.float32)
    parent_beam = draw_parent_beam(jax.random.fold_in(jax.random.fold_in(key_of[6], part), 71), part)
    next_token = plant(ranked_ids(part_keys[2], (HYPS,), VOCAB, 2), jax.random.fold_in(part_keys[2], 3), 0, VOCAB - 1).astype(jnp.int32)
    proj_table = gaussian(key_of[3], (VOCAB, HEADS, 5 * HEAD_DIM), 1.0, 6.0, ((0, 8), (1, 2)))
    gate_table = gaussian(key_of[4], (VOCAB, 3, HEADS), 1.5, 6.0, ((0, 8), (2, 2)))
    gain = jnp.clip(1.0 + 0.18 * jax.random.normal(key_of[5], (HEADS, HEAD_DIM), jnp.float32), 0.1, 1.9)
    return dict(states=states, parent_beam=parent_beam, next_token=next_token, proj_table=proj_table, gate_table=gate_table, gain=gain)


def unit_norm(vector):
    return vector * lax.rsqrt(lax.optimization_barrier(jnp.sum(vector * vector, axis=-1, keepdims=True)) + 1e-06)

def advance(parents, entries, gate_entries, gain):
    retain = jax.nn.sigmoid(gate_entries[:, 0, :])
    strengths = 2.0 * jax.nn.sigmoid(gate_entries[:, 1:, :])
    state_now = retain[:, :, None, None] * parents
    for reflect in range(2):
        key_unit = unit_norm(entries[:, :, 1 + reflect, :])
        value_row = entries[:, :, 3 + reflect, :]
        applied = jnp.einsum('nhvd,nhd->nhv', state_now, key_unit, precision=lax.Precision.HIGHEST)
        state_now = state_now - strengths[:, reflect, :, None, None] * (applied - value_row)[:, :, :, None] * key_unit[:, :, None, :]
    query_unit = unit_norm(entries[:, :, 0, :])
    readout = jnp.einsum('nhvd,nhd->nhv', state_now, query_unit, precision=lax.Precision.HIGHEST)
    normed = gain[None, :, :] * readout * lax.rsqrt(lax.optimization_barrier(jnp.mean(readout * readout, axis=-1, keepdims=True)) + 1e-05)
    return (normed.astype(jnp.bfloat16), state_now)

def reference(states, parent_beam, next_token, proj_table, gate_table, gain):
    hyp_index = jnp.arange(HYPS, dtype=jnp.int32)
    utterance = hyp_index % UTTS
    parent_hyp = (parent_beam * UTTS + utterance).astype(jnp.int32)
    parents = states[parent_hyp]
    entries = proj_table[next_token].astype(jnp.float32).reshape(HYPS, HEADS, 5, HEAD_DIM)
    gate_entries = gate_table[next_token].astype(jnp.float32)
    return advance(parents, entries, gate_entries, gain)
```

```python
import jax
import jax.numpy as jnp
from jax import lax
from jax.sharding import PartitionSpec as P

HEAD_DIM = 128
BEAMS = 8
FAR, NEAR, SIDE = 4, 2, 1
WIRE = jnp.float16
CHUNKS = 2


def swap(block, mask):
    devices = lax.axis_size("beam")
    spacing = devices // BEAMS
    route = [(i, ((i // spacing) ^ mask) * spacing + i % spacing) for i in range(devices)]
    return lax.ppermute(block, "beam", route)


def unit_norm(vector):
    return vector * lax.rsqrt(jnp.sum(vector * vector, axis=-1, keepdims=True) + 1e-06)


def advance(parents, entries, gate_entries, gain):
    retain = jax.nn.sigmoid(gate_entries[:, 0, :])
    strengths = 2.0 * jax.nn.sigmoid(gate_entries[:, 1:, :])
    state_now = retain[:, :, None, None] * parents
    for reflect in range(2):
        key_unit = unit_norm(entries[:, :, 1 + reflect, :])
        value_row = entries[:, :, 3 + reflect, :]
        applied = jnp.einsum("nhvd,nhd->nhv", state_now, key_unit, precision=lax.Precision.HIGHEST)
        state_now = (
            state_now
            - strengths[:, reflect, :, None, None]
            * (applied - value_row)[:, :, :, None]
            * key_unit[:, :, None, :]
        )
    query_unit = unit_norm(entries[:, :, 0, :])
    readout = jnp.einsum("nhvd,nhd->nhv", state_now, query_unit, precision=lax.Precision.HIGHEST)
    normed = (
        gain[None, :, :]
        * readout
        * lax.rsqrt(jnp.mean(readout * readout, axis=-1, keepdims=True) + 1e-05)
    )
    return (normed.astype(jnp.bfloat16), state_now)


def look_up(next_token, proj_table, gate_table):
    hyp_rows = next_token.shape[0]
    devices = lax.axis_size("beam")
    vocab_rows, head_count = proj_table.shape[:2]
    tokens = lax.all_to_all(
        jnp.broadcast_to(next_token[None, :], (devices, hyp_rows)), "beam", 0, 0, tiled=True
    ).reshape(devices * hyp_rows)
    local_ids = tokens - lax.axis_index("beam") * vocab_rows
    onehot = (local_ids[:, None] == jnp.arange(vocab_rows, dtype=jnp.int32)[None, :]).astype(
        jnp.bfloat16
    )
    width = head_count * 5 * HEAD_DIM
    looked = jnp.dot(
        onehot, proj_table.reshape(vocab_rows, width), preferred_element_type=jnp.float32
    ).astype(jnp.bfloat16)
    looked_gates = jnp.dot(
        onehot, gate_table.reshape(vocab_rows, 3 * head_count), preferred_element_type=jnp.float32
    ).astype(jnp.bfloat16)
    rows = jnp.concatenate([looked, looked_gates], axis=1).reshape(devices, hyp_rows, -1)
    arrived = lax.all_to_all(rows, "beam", split_axis=0, concat_axis=0, tiled=True)
    summed = jnp.sum(arrived, axis=0, dtype=jnp.float32)
    entries = summed[:, :width].reshape(hyp_rows, head_count, 5, HEAD_DIM)
    gate_entries = summed[:, width:].reshape(hyp_rows, 3, head_count)
    return entries, gate_entries


def pick(near, far, far_side, side, relation):
    rel = relation[:, None, None, None]
    return jnp.where(
        (rel & FAR) != 0,
        jnp.where((rel & SIDE) != 0, far_side, far),
        jnp.where((rel & SIDE) != 0, side, near),
    )


def local(states, parent_beam, next_token, proj_table, gate_table, gain):
    devices = lax.axis_size("beam")
    my_beam = lax.axis_index("beam") // (devices // BEAMS)
    relation = parent_beam ^ my_beam
    peer_relation = swap(parent_beam, NEAR) ^ my_beam
    entries, gate_entries = look_up(next_token, proj_table, gate_table)
    head_count = states.shape[1]
    step = head_count // CHUNKS
    parents = []
    for chunk in range(CHUNKS):
        exact = states[:, chunk * step : (chunk + 1) * step]
        near = exact.astype(WIRE)
        far = swap(near, FAR)
        side = swap(near, SIDE)
        far_side = swap(far, SIDE)
        block = swap(pick(near, far, far_side, side, peer_relation), NEAR)
        mine = pick(
            exact,
            far.astype(jnp.float32),
            far_side.astype(jnp.float32),
            side.astype(jnp.float32),
            relation,
        )
        crossed = (relation & NEAR)[:, None, None, None] != 0
        parents.append(jnp.where(crossed, block.astype(jnp.float32), mine))
    return advance(jnp.concatenate(parents, axis=1), entries, gate_entries, gain)


def solution(mesh):
    return jax.shard_map(
        local,
        mesh=mesh,
        in_specs=(
            P(("groups", "beam"), "mp", None, None),
            P(("groups", "beam")),
            P(("groups", "beam")),
            P("beam", "mp", None),
            P("beam", None, "mp"),
            P("mp", None),
        ),
        out_specs=(P(("groups", "beam"), "mp", None), P(("groups", "beam"), "mp", None, None)),
        check_vma=False,
    )
```

```python
import jax
import jax.numpy as jnp
from jax import lax
from jax.experimental import pallas as pl
from jax.sharding import PartitionSpec as P

HEAD_DIM = 128
BEAMS = 8
FAR, NEAR, SIDE = 4, 2, 1
WIRE = jnp.float16
PARTS = (2, 2)


def swap(block, mask):
    devices = lax.axis_size("beam")
    spacing = devices // BEAMS
    route = [(i, ((i // spacing) ^ mask) * spacing + i % spacing) for i in range(devices)]
    return lax.ppermute(block, "beam", route)


def exchange(block):
    return lax.all_to_all(block, "beam", split_axis=0, concat_axis=0, tiled=True)


def unit_norm(vector):
    return vector * lax.rsqrt(jnp.sum(vector * vector, axis=-1, keepdims=True) + 1e-06)


def pack_vectors(entries, gate_entries):
    units = unit_norm(entries[:, :, :3, :])
    gates = jnp.swapaxes(jax.nn.sigmoid(gate_entries), 1, 2)
    gates = gates * jnp.array([1.0, 2.0, 2.0], jnp.float32)
    gates = jnp.broadcast_to(gates[:, :, :, None], gates.shape + (HEAD_DIM,))
    return jnp.concatenate([units, entries[:, :, 3:, :], gates], axis=2)


def next_head(refs, row, head):
    for ref in refs:
        if head < ref.shape[1]:
            return ref[row, head]
        head -= ref.shape[1]


def column_sum(block):
    return jnp.sum(block, axis=1, keepdims=True)


def advance_body(*refs):
    vectors_ref, gain_ref, *parent_refs, readout_ref, states_ref = refs
    rows, heads = states_ref.shape[:2]
    shape = (HEAD_DIM, HEAD_DIM)
    diagonal = lax.broadcasted_iota(jnp.int32, shape, 0) == lax.broadcasted_iota(jnp.int32, shape, 1)
    for row in range(rows):
        outs = []
        for head in range(heads):
            vecs = vectors_ref[row, head]
            parent = next_head(parent_refs, row, head)
            query, key1, key2 = vecs[0:1], vecs[1:2], vecs[2:3]
            value1, value2 = vecs[3:4], vecs[4:5]
            beta1, beta2 = vecs[6:7, 0:1], vecs[7:8, 0:1]
            state = vecs[5:6] * parent
            part = state * key1
            step1 = beta1 * column_sum(jnp.where(diagonal, part - value1, part))
            state = state - step1 * key1
            part = state * key2
            step2 = beta2 * column_sum(jnp.where(diagonal, part - value2, part))
            state = state - step2 * key2
            states_ref[row, head] = state
            out = column_sum(state * query)
            outs.append(jnp.sum(jnp.where(diagonal, out, 0.0), axis=0, keepdims=True))
        out = jnp.concatenate(outs, axis=0)
        scale = lax.rsqrt(jnp.mean(out * out, axis=1, keepdims=True) + 1e-05)
        readout_ref[row] = (gain_ref[...] * out * scale).astype(readout_ref.dtype)


def advance(parents, entries, gate_entries, gain):
    rows = parents[0].shape[0]
    heads = gain.shape[0]
    return pl.pallas_call(
        advance_body,
        out_shape=(
            jax.ShapeDtypeStruct((rows, heads, HEAD_DIM), jnp.bfloat16),
            jax.ShapeDtypeStruct((rows, heads, HEAD_DIM, HEAD_DIM), jnp.float32),
        ),
        name="advance",
    )(pack_vectors(entries, gate_entries), gain, *parents)


def look_up(next_token, proj_table, gate_table):
    hyp_rows = next_token.shape[0]
    devices = lax.axis_size("beam")
    vocab_rows, head_count = proj_table.shape[:2]
    tokens = exchange(
        jnp.broadcast_to(next_token[None, :], (devices, hyp_rows))
    ).reshape(devices * hyp_rows)
    local_ids = tokens - lax.axis_index("beam") * vocab_rows
    onehot = (local_ids[:, None] == jnp.arange(vocab_rows, dtype=jnp.int32)[None, :]).astype(
        jnp.bfloat16
    )
    width = head_count * 5 * HEAD_DIM
    looked = jnp.dot(
        onehot, proj_table.reshape(vocab_rows, width), preferred_element_type=jnp.float32
    ).astype(jnp.bfloat16)
    looked_gates = jnp.dot(
        onehot, gate_table.reshape(vocab_rows, 3 * head_count), preferred_element_type=jnp.float32
    ).astype(jnp.bfloat16)
    rows = jnp.concatenate([looked, looked_gates], axis=1).reshape(devices, hyp_rows, -1)
    arrived = exchange(rows)
    summed = jnp.sum(arrived, axis=0, dtype=jnp.float32)
    entries = summed[:, :width].reshape(hyp_rows, head_count, 5, HEAD_DIM)
    gate_entries = summed[:, width:].reshape(hyp_rows, 3, head_count)
    return entries, gate_entries


def pick(near, far, far_side, side, relation):
    rel = relation[:, None, None, None]
    return jnp.where(
        (rel & FAR) != 0,
        jnp.where((rel & SIDE) != 0, far_side, far),
        jnp.where((rel & SIDE) != 0, side, near),
    )


def step(states, parent_beam, next_token, proj_table, gate_table, gain):
    devices = lax.axis_size("beam")
    my_beam = lax.axis_index("beam") // (devices // BEAMS)
    relation = parent_beam ^ my_beam
    peer_relation = swap(parent_beam, NEAR) ^ my_beam
    entries, gate_entries = look_up(next_token, proj_table, gate_table)
    head_count = states.shape[1]
    unit = head_count // sum(PARTS)
    crossed = (relation & NEAR)[:, None, None, None] != 0
    parents = []
    start = 0
    for part in PARTS:
        exact = states[:, start : start + part * unit]
        start += part * unit
        near = exact.astype(WIRE)
        far = swap(near, FAR)
        side = swap(near, SIDE)
        far_side = swap(far, SIDE)
        block = swap(pick(near, far, far_side, side, peer_relation), NEAR)
        mine = pick(
            exact,
            far.astype(jnp.float32),
            far_side.astype(jnp.float32),
            side.astype(jnp.float32),
            relation,
        )
        parents.append(jnp.where(crossed, block.astype(jnp.float32), mine))
    return advance(parents, entries, gate_entries, gain)


def solution(mesh):
    return jax.shard_map(
        step,
        mesh=mesh,
        in_specs=(
            P(("groups", "beam"), "mp", None, None),
            P(("groups", "beam")),
            P(("groups", "beam")),
            P("beam", "mp", None),
            P("beam", None, "mp"),
            P("mp", None),
        ),
        out_specs=(P(("groups", "beam"), "mp", None), P(("groups", "beam"), "mp", None, None)),
        check_vma=False,
    )
```

```python
import jax
import jax.numpy as jnp
from jax import lax
from jax.experimental import pallas as pl
from jax.sharding import PartitionSpec as P

HEAD_DIM = 128
BEAMS = 8
FAR, NEAR, SIDE = 4, 2, 1
WIRE = jnp.float16
PARTS = (2, 2)


def swap(block, mask):
    devices = lax.axis_size("beam")
    spacing = devices // BEAMS
    route = [(i, ((i // spacing) ^ mask) * spacing + i % spacing) for i in range(devices)]
    return lax.ppermute(block, "beam", route)


def exchange(block):
    return lax.all_to_all(block, "beam", split_axis=0, concat_axis=0, tiled=True)


def unit_norm(vector):
    return vector * lax.rsqrt(jnp.sum(vector * vector, axis=-1, keepdims=True) + 1e-06)


def pack_vectors(entries, gate_entries):
    units = unit_norm(entries[:, :, :3, :])
    gates = jnp.swapaxes(jax.nn.sigmoid(gate_entries), 1, 2)
    gates = gates * jnp.array([1.0, 2.0, 2.0], jnp.float32)
    gates = jnp.broadcast_to(gates[:, :, :, None], gates.shape + (HEAD_DIM,))
    return jnp.concatenate([units, entries[:, :, 3:, :], gates], axis=2)


def next_head(refs, row, head):
    for ref in refs:
        if head < ref.shape[1]:
            return ref[row, head]
        head -= ref.shape[1]


def split(block):
    high = block.astype(jnp.bfloat16)
    return high, (block - high.astype(jnp.float32)).astype(jnp.bfloat16)


def dot(left, right, axis):
    return lax.dot_general(
        left, right, (((axis,), (axis,)), ((), ())), preferred_element_type=jnp.float32
    )


def advance_body(*refs):
    vectors_ref, gain_ref, *parent_refs, readout_ref, states_ref = refs
    rows, heads = states_ref.shape[:2]
    applied = {}
    for row in range(rows):
        for head in range(heads):
            high, low = split(vectors_ref[row, head])
            both = jnp.concatenate([high, low], axis=0)
            parent_high, parent_low = split(next_head(parent_refs, row, head))
            product = dot(both, parent_high, 1) + dot(both, parent_low, 1)
            applied[row, head] = product[:8] + product[8:]
    updates = {}
    for row in range(rows):
        outs = []
        for head in range(heads):
            vecs = vectors_ref[row, head]
            seen = vecs[5:6] * applied[row, head]
            query, key1, key2 = vecs[0:1], vecs[1:2], vecs[2:3]
            across = jnp.sum(key1 * key2, axis=1, keepdims=True)
            from1 = jnp.sum(key1 * query, axis=1, keepdims=True)
            from2 = jnp.sum(key2 * query, axis=1, keepdims=True)
            step1 = vecs[6:7] * (seen[1:2] - vecs[3:4])
            step2 = vecs[7:8] * (seen[2:3] - step1 * across - vecs[4:5])
            outs.append(seen[0:1] - step1 * from1 - step2 * from2)
            steps = jnp.concatenate([step1, step2], axis=0)
            updates[row, head] = steps
        out = jnp.concatenate(outs, axis=0)
        scale = lax.rsqrt(jnp.mean(out * out, axis=1, keepdims=True) + 1e-05)
        readout_ref[row] = (gain_ref[...] * out * scale).astype(readout_ref.dtype)
    blank = jnp.zeros((2, HEAD_DIM), jnp.float32)
    for row in range(rows):
        for head in range(heads):
            vecs = vectors_ref[row, head]
            steps = updates[row, head]
            keys = vecs[1:3]
            steps_high = steps.astype(jnp.bfloat16).astype(jnp.float32)
            keys_high = keys.astype(jnp.bfloat16).astype(jnp.float32)
            left = jnp.concatenate([steps_high, steps - steps_high, steps_high, blank], axis=0)
            right = jnp.concatenate([keys_high, keys_high, keys - keys_high, blank], axis=0)
            moved = dot(left.astype(jnp.bfloat16), right.astype(jnp.bfloat16), 0)
            states_ref[row, head] = vecs[5:6] * next_head(parent_refs, row, head) - moved


def advance(parents, entries, gate_entries, gain):
    rows = parents[0].shape[0]
    heads = gain.shape[0]
    return pl.pallas_call(
        advance_body,
        out_shape=(
            jax.ShapeDtypeStruct((rows, heads, HEAD_DIM), jnp.bfloat16),
            jax.ShapeDtypeStruct((rows, heads, HEAD_DIM, HEAD_DIM), jnp.float32),
        ),
        name="advance",
    )(pack_vectors(entries, gate_entries), gain, *parents)


def look_up(next_token, proj_table, gate_table):
    hyp_rows = next_token.shape[0]
    devices = lax.axis_size("beam")
    vocab_rows, head_count = proj_table.shape[:2]
    tokens = exchange(
        jnp.broadcast_to(next_token[None, :], (devices, hyp_rows))
    ).reshape(devices * hyp_rows)
    local_ids = tokens - lax.axis_index("beam") * vocab_rows
    onehot = (local_ids[:, None] == jnp.arange(vocab_rows, dtype=jnp.int32)[None, :]).astype(
        jnp.bfloat16
    )
    width = head_count * 5 * HEAD_DIM
    looked = jnp.dot(
        onehot, proj_table.reshape(vocab_rows, width), preferred_element_type=jnp.float32
    ).astype(jnp.bfloat16)
    looked_gates = jnp.dot(
        onehot, gate_table.reshape(vocab_rows, 3 * head_count), preferred_element_type=jnp.float32
    ).astype(jnp.bfloat16)
    rows = jnp.concatenate([looked, looked_gates], axis=1).reshape(devices, hyp_rows, -1)
    arrived = exchange(rows)
    summed = jnp.sum(arrived, axis=0, dtype=jnp.float32)
    entries = summed[:, :width].reshape(hyp_rows, head_count, 5, HEAD_DIM)
    gate_entries = summed[:, width:].reshape(hyp_rows, 3, head_count)
    return entries, gate_entries


def pick(near, far, far_side, side, relation):
    rel = relation[:, None, None, None]
    return jnp.where(
        (rel & FAR) != 0,
        jnp.where((rel & SIDE) != 0, far_side, far),
        jnp.where((rel & SIDE) != 0, side, near),
    )


def step(states, parent_beam, next_token, proj_table, gate_table, gain):
    devices = lax.axis_size("beam")
    my_beam = lax.axis_index("beam") // (devices // BEAMS)
    relation = parent_beam ^ my_beam
    peer_relation = swap(parent_beam, NEAR) ^ my_beam
    entries, gate_entries = look_up(next_token, proj_table, gate_table)
    head_count = states.shape[1]
    unit = head_count // sum(PARTS)
    crossed = (relation & NEAR)[:, None, None, None] != 0
    parents = []
    start = 0
    for part in PARTS:
        exact = states[:, start : start + part * unit]
        start += part * unit
        near = exact.astype(WIRE)
        far = swap(near, FAR)
        side = swap(near, SIDE)
        far_side = swap(far, SIDE)
        block = swap(pick(near, far, far_side, side, peer_relation), NEAR)
        mine = pick(
            exact,
            far.astype(jnp.float32),
            far_side.astype(jnp.float32),
            side.astype(jnp.float32),
            relation,
        )
        parents.append(jnp.where(crossed, block.astype(jnp.float32), mine))
    return advance(parents, entries, gate_entries, gain)


def solution(mesh):
    return jax.shard_map(
        step,
        mesh=mesh,
        in_specs=(
            P(("groups", "beam"), "mp", None, None),
            P(("groups", "beam")),
            P(("groups", "beam")),
            P("beam", "mp", None),
            P("beam", None, "mp"),
            P("mp", None),
        ),
        out_specs=(P(("groups", "beam"), "mp", None), P(("groups", "beam"), "mp", None, None)),
        check_vma=False,
    )
```
